256 devices in a mesh: grp: 8 (over z), sp: 32 (over y, x, core).
Axes of the slice: x: 4, y: 4, z: 8, core: 2. Of those that a mesh axis runs over, the one named last changes fastest.
Arguments:
- queries: bfloat16 [65536, 4096], P(('grp', 'sp')), may hold values from -48 to 48
- keys: bfloat16 [65536, 4096], P(('grp', 'sp')), may hold values from -48 to 48
- values: bfloat16 [65536, 4096], P(('grp', 'sp')), may hold values from -6 to 6
- clip_lengths: int32 [8, 16], P('grp'), may hold values from 1 to 1023, as said below
- clip_plan: int32 [8, 16], P('grp'), may hold values from 0 to 7
Outputs:
- attended: bfloat16 [65536, 4096], P(('grp', 'sp'))
The draws below stay inside these ranges and needn't reach their ends.
Inputs may be any that keep to these rules, and one draw needn't show every extreme that they name: `clip_lengths`: each group's clips, in order, fill its 8192 source rows; the clips that one group sends to any one group are exactly 2 and hold exactly 1024 frames together.
All inputs are finite; a program needn't handle non-finite values.
Results may differ from the reference program's by a relative error of at most 0.0037.
Values may be sent and summed in bfloat16 or wider, within the bound.
A program may use at most 64 MiB of HBM per device.

```python
import math
from functools import partial
import jax
import jax.numpy as jnp
from jax import lax

HEAD_COUNT = 32
HEAD_DIM = 128
MODEL_WIDTH = 4096
CLIP_SHARE = 2
GROUP_COUNT = 8
SHARE_FRAMES = 1024
ALL_FRAMES = 65536


def clip_tables_draw(key):
    group_count = GROUP_COUNT
    portion_count = group_count * group_count
    base = jax.random.fold_in(key, 17)
    cut_key = jax.random.fold_in(base, 1)
    order_key = jax.random.fold_in(base, 2)
    pick_key = jax.random.fold_in(base, 3)

    def composition(sub_key):
        cut_points = jax.random.permutation(sub_key, SHARE_FRAMES - 1)[:CLIP_SHARE - 1] + 1
        cut_points = jnp.sort(cut_points.astype(jnp.int32))
        boundaries = jnp.concatenate([jnp.zeros((1,), jnp.int32), cut_points, jnp.full((1,), SHARE_FRAMES, jnp.int32)])
        return boundaries[1:] - boundaries[:-1]
    pieces = jax.vmap(composition)(jax.random.split(cut_key, portion_count))
    forced = jnp.concatenate([jnp.full((1,), SHARE_FRAMES - CLIP_SHARE + 1, jnp.int32), jnp.ones((CLIP_SHARE - 1,), jnp.int32)])
    chosen_portion = jax.random.randint(pick_key, (), 0, portion_count)
    pieces = jnp.where((jnp.arange(portion_count) == chosen_portion)[:, None], forced[None, :], pieces)
    lengths = pieces.reshape(group_count, group_count * CLIP_SHARE)
    destination = jnp.repeat(jnp.arange(group_count, dtype=jnp.int32), CLIP_SHARE)
    destination = jnp.broadcast_to(destination[None, :], (group_count, group_count * CLIP_SHARE))

    def shuffle(sub_key):
        return jax.random.permutation(sub_key, group_count * CLIP_SHARE)
    orders = jax.vmap(shuffle)(jax.random.split(order_key, group_count))
    lengths = jnp.take_along_axis(lengths, orders, axis=1)
    destination = jnp.take_along_axis(destination, orders, axis=1)
    return (lengths.astype(jnp.int32), destination.astype(jnp.int32))


def draw_clip_lengths(key, part):
    return clip_tables_draw(key)[0]


def draw_clip_plan(key, part):
    return clip_tables_draw(key)[1]


def draw_queries(key, part):
    shape = (ALL_FRAMES, MODEL_WIDTH)
    result = jnp.clip(jax.random.normal(jax.random.fold_in(key, 3), shape, jnp.float32), -6.0, 6.0)
    return jnp.clip(result, -48.0, 48.0).astype(jnp.bfloat16)


def draw_keys(key, part):
    shape = (ALL_FRAMES, MODEL_WIDTH)
    result = jnp.clip(jax.random.normal(jax.random.fold_in(key, 4), shape, jnp.float32), -6.0, 6.0)
    return jnp.clip(result, -48.0, 48.0).astype(jnp.bfloat16)


def levels(key, extent, cuts, least, high):
    loudness = 1.0
    for axis_at, shards_of in cuts:
        steps = jax.random.uniform(jax.random.fold_in(jax.random.fold_in(key, 6), axis_at), (shards_of,), jnp.float32, least / len(cuts), high / len(cuts))
        loudness = loudness * jnp.repeat(jnp.exp(steps), extent[axis_at] // shards_of).reshape((-1,) + (1,) * (len(extent) - 1 - axis_at))
    return loudness


def gaussian(stream_key, shape, scale, most, cuts=(), kind=jnp.bfloat16):
    drawn = scale * jax.random.normal(stream_key, shape, jnp.float32)
    if cuts:
        drawn = drawn * levels(stream_key, shape, cuts, -0.22, 0.18)
    return jnp.clip(drawn, -most, most).astype(kind)


def setup_inputs(seed: int = 0) -> dict:
    seeds = jax.random.split(jax.random.key(seed), 6)
    queries = draw_queries(jax.random.fold_in(seeds[5], 71), 0)
    keys = draw_keys(jax.random.fold_in(seeds[5], 71), 0)
    values = gaussian(seeds[2], (ALL_FRAMES, MODEL_WIDTH), 1.0, 6.0, ((0, 256),))
    clip_lengths = draw_clip_lengths(jax.random.fold_in(seeds[5], 71), 0)
    clip_plan = draw_clip_plan(jax.random.fold_in(seeds[5], 71), 0)
    return dict(queries=queries, keys=keys, values=values, clip_lengths=clip_lengths, clip_plan=clip_plan)


def row_tables(lengths, destination, frames):
    clip_order = jnp.arange(lengths.shape[0], dtype=jnp.int32)
    earlier = clip_order[None, :] < clip_order[:, None]
    clip_start = lax.optimization_barrier(jnp.sum(jnp.where(earlier, lengths[None, :], 0), axis=1)).astype(jnp.int32)
    before = (destination[None, :] < destination[:, None]) | (destination[None, :] == destination[:, None]) & earlier
    sorted_start = lax.optimization_barrier(jnp.sum(jnp.where(before, lengths[None, :], 0), axis=1)).astype(jnp.int32)
    positions = jnp.arange(frames, dtype=jnp.int32)[:, None]
    inside_sorted = (positions >= sorted_start[None, :]) & (positions < (sorted_start + lengths)[None, :])
    source_row = lax.optimization_barrier(jnp.sum(jnp.where(inside_sorted, clip_start[None, :] + positions - sorted_start[None, :], 0), axis=1)).astype(jnp.int32)
    sorted_begin = lax.optimization_barrier(jnp.sum(jnp.where(inside_sorted, sorted_start[None, :], 0), axis=1)).astype(jnp.int32)
    inside_source = (positions >= clip_start[None, :]) & (positions < (clip_start + lengths)[None, :])
    source_begin = lax.optimization_barrier(jnp.sum(jnp.where(inside_source, clip_start[None, :], 0), axis=1)).astype(jnp.int32)
    return (source_row, sorted_begin, source_begin)

def attend_portions(query_all, key_all, value_all, clip_begin):
    share_rows = query_all.shape[1]
    tile_rows = share_rows // 4
    score_scale = 1.0 / math.sqrt(HEAD_DIM)
    pieces = []
    for tile_index in range(4):
        tile_first = tile_index * tile_rows
        tile_last = tile_first + tile_rows
        query_tile = query_all[:, tile_first:tile_last]
        key_tile = key_all[:, :tile_last]
        value_tile = value_all[:, :tile_last]
        scores = jnp.einsum('pqnd,pknd->pnqk', query_tile, key_tile) * score_scale
        query_pos = jnp.arange(tile_first, tile_last, dtype=jnp.int32)
        key_pos = jnp.arange(tile_last, dtype=jnp.int32)
        allowed = (key_pos[None, None, :] >= clip_begin[:, tile_first:tile_last, None]) & (key_pos[None, None, :] <= query_pos[None, :, None])
        scores = jnp.where(allowed[:, None], scores, -jnp.inf)
        highest = lax.optimization_barrier(jnp.max(scores, axis=-1, keepdims=True))
        weights = jnp.exp(scores - highest)
        totals = lax.optimization_barrier(jnp.sum(weights, axis=-1))
        rounded = lax.optimization_barrier(weights.astype(jnp.bfloat16))
        mixture = jnp.einsum('pnqk,pknd->pqnd', rounded.astype(jnp.float32), value_tile)
        pieces.append(mixture / jnp.transpose(totals, (0, 2, 1))[..., None])
    return jnp.concatenate(pieces, axis=1)

def reference(queries, keys, values, clip_lengths, clip_plan):
    group_count = clip_lengths.shape[0]
    frames = queries.shape[0] // group_count
    share_rows = frames // group_count
    tables = jax.vmap(partial(row_tables, frames=frames))(clip_lengths, clip_plan)
    groups = jnp.arange(group_count, dtype=jnp.int32)
    source_rows = tables[0].reshape(group_count, group_count, share_rows) + (groups * frames)[:, None, None]
    begins = tables[1].reshape(group_count, group_count, share_rows) - (groups * share_rows)[None, :, None]
    source_rows = jnp.transpose(source_rows, (1, 0, 2)).reshape(group_count, frames)
    begins = jnp.transpose(begins, (1, 0, 2))

    def one_group(item):
        row_index, clip_begin = item

        def placed(array):
            return jnp.take(array, row_index, axis=0).astype(jnp.float32).reshape(group_count, share_rows, HEAD_COUNT, HEAD_DIM)
        mixture = attend_portions(placed(queries), placed(keys), placed(values), clip_begin)
        return mixture.reshape(frames, MODEL_WIDTH).astype(jnp.bfloat16)
    attended = lax.map(one_group, (source_rows, begins))
    return attended.reshape(group_count * frames, MODEL_WIDTH)
```

```python
import functools
import math

import jax
import jax.numpy as jnp
from jax import lax
from jax.experimental import pallas as pl
from jax.experimental.pallas import tpu as pltpu
from jax.sharding import PartitionSpec as P

HEAD_DIM = 128
MESH = pl.DeviceIdType.MESH
STRIDE = 11
MASKED = -1.0e30


def fused_kernel(
    groups,
    sp_size,
    lens_ref,
    plan_ref,
    q_hbm,
    k_hbm,
    v_hbm,
    out_hbm,
    q_all,
    k_all,
    v_all,
    begin_all,
    prob_all,
    inverse_all,
    mixed_all,
    sorted_all,
    placed_all,
    in_send,
    in_recv,
    z_send,
    z_recv,
    out_send,
    out_recv,
    own_sem,
):
    rows = q_hbm.shape[0]
    clips = lens_ref.shape[1]
    quarters = sp_size // groups
    share = rows * quarters
    frames = rows * sp_size
    window = share + rows
    group = lax.axis_index("grp")
    me = lax.axis_index("sp")

    barrier = pltpu.get_barrier_semaphore()

    @pl.loop(1, sp_size)
    def _(t):
        peer = lax.rem(me + t, sp_size)
        pl.semaphore_signal(barrier, inc=1, device_id=(group, peer), device_id_type=MESH)

    @pl.loop(1, groups)
    def _(t):
        peer = lax.rem(group + t, groups)
        pl.semaphore_signal(barrier, inc=1, device_id=(peer, me), device_id_type=MESH)

    pl.semaphore_wait(barrier, sp_size + groups - 2)

    def head_columns(array, head):
        return array.at[:, pl.ds(pl.multiple_of(head * HEAD_DIM, HEAD_DIM), HEAD_DIM)]

    stacks = ((k_hbm, k_all, quarters), (q_hbm, q_all, 0), (v_hbm, v_all, quarters))

    def send_head(index, head):
        source, stack, pad = stacks[index]
        pltpu.make_async_remote_copy(
            src_ref=head_columns(source, head),
            dst_ref=stack.at[pad + me],
            send_sem=in_send.at[index],
            recv_sem=in_recv.at[index, me],
            device_id=(group, head),
            device_id_type=MESH,
        ).start()

    for index in range(3):
        source, stack, pad = stacks[index]
        pltpu.make_async_copy(
            head_columns(source, me), stack.at[pad + me], in_recv.at[index, me]
        ).start()

    @pl.loop(1, sp_size)
    def _(t):
        head = lax.rem(me + t * STRIDE, sp_size)
        send_head(0, head)
        send_head(1, head)

    @pl.loop(1, sp_size)
    def _(t):
        send_head(2, lax.rem(me + t * STRIDE, sp_size))

    def wait_block(index, block):
        _, stack, pad = stacks[index]
        view = stack.at[pad + block]
        pltpu.make_async_copy(view, view, in_recv.at[index, block]).wait()

    lengths = [lens_ref[0, c] for c in range(clips)]
    plans = [plan_ref[0, c] for c in range(clips)]
    starts = []
    total = jnp.int32(0)
    for c in range(clips):
        starts.append(total)
        total = total + lengths[c]

    k_all[0:quarters] = jnp.zeros((quarters, rows, HEAD_DIM), k_all.dtype)
    v_all[0:quarters] = jnp.zeros((quarters, rows, HEAD_DIM), v_all.dtype)
    mixed_all[0:share, :] = jnp.zeros((share, HEAD_DIM), jnp.float32)
    mixed_all[share + frames :, :] = jnp.zeros((share, HEAD_DIM), jnp.float32)

    @pl.loop(0, sp_size)
    def _(block):
        first = block * rows
        position = first + lax.broadcasted_iota(jnp.int32, (rows, HEAD_DIM), 0)
        begin = jnp.zeros((rows, HEAD_DIM), jnp.int32)
        for c in range(1, clips):
            begin = jnp.where(position >= starts[c], starts[c], begin)
        begin_all[block] = begin - (first - share)

    scale = math.log2(math.e) / math.sqrt(HEAD_DIM)
    column = lax.broadcasted_iota(jnp.int32, (rows, window), 1)
    last_key = share + lax.broadcasted_iota(jnp.int32, (rows, window), 0)

    @pl.loop(0, sp_size)
    def _(block):
        wait_block(0, block)
        wait_block(1, block)
        window_keys = k_all[pl.ds(block, quarters + 1)].reshape(window, HEAD_DIM)
        scores = lax.dot_general(
            q_all[block],
            window_keys,
            (((1,), (1,)), ((), ())),
            preferred_element_type=jnp.float32,
        )
        begin = jnp.broadcast_to(begin_all[block][:, :1], (rows, window))
        allowed = (column >= begin) & (column <= last_key)
        scores = jnp.where(allowed, scores * scale, MASKED)
        highest = jnp.max(scores, axis=1, keepdims=True)
        weights = jnp.exp2(scores - highest)
        totals = jnp.sum(weights, axis=1, keepdims=True)
        inverse_all[block] = jnp.broadcast_to(1.0 / totals, (rows, HEAD_DIM))
        prob_all[block] = weights.astype(prob_all.dtype)

    @pl.loop(0, sp_size)
    def _(block):
        wait_block(2, block)
        window_values = v_all[pl.ds(block, quarters + 1)].reshape(window, HEAD_DIM)
        mixture = jnp.dot(prob_all[block], window_values, preferred_element_type=jnp.float32)
        mixed_all[pl.ds(pl.multiple_of(share + block * rows, rows), rows), :] = (
            mixture * inverse_all[block]
        )

    def pair_of(target):
        first_start = jnp.int32(0)
        first_length = jnp.int32(0)
        second_start = jnp.int32(0)
        for c in reversed(range(clips)):
            hit = plans[c] == target
            first_start = jnp.where(hit, starts[c], first_start)
            first_length = jnp.where(hit, lengths[c], first_length)
        for c in range(clips):
            second_start = jnp.where(plans[c] == target, starts[c], second_start)
        return first_start, first_length, second_start

    def step_of(step):
        quarter = lax.rem(step // groups + me, quarters)
        shift = lax.rem(5 * lax.rem(step, groups) + groups // 2, groups)
        return quarter, shift

    def z_copy(target, quarter):
        return pltpu.make_async_remote_copy(
            src_ref=sorted_all.at[target, quarter],
            dst_ref=placed_all.at[group, quarter],
            send_sem=z_send,
            recv_sem=z_recv.at[group, quarter],
            device_id=(target, me),
            device_id_type=MESH,
        )

    def deliver(block_ref, origin, quarter):
        holder = origin * quarters + quarter
        target = head_columns(out_hbm, me)

        @pl.when(holder == me)
        def _():
            pltpu.make_async_copy(block_ref, target, own_sem).start()

        @pl.when(holder != me)
        def _():
            pltpu.make_async_remote_copy(
                src_ref=block_ref,
                dst_ref=target,
                send_sem=out_send,
                recv_sem=out_recv,
                device_id=(group, holder),
                device_id_type=MESH,
            ).start()

    @pl.loop(0, groups * quarters)
    def _(step):
        quarter, shift = step_of(step)
        target = lax.rem(group + shift, groups)
        first_start, first_length, second_start = pair_of(target)
        offset = quarter * rows
        head = mixed_all[pl.ds(share + first_start + offset, rows), :]
        tail = mixed_all[pl.ds(share + second_start - first_length + offset, rows), :]
        position = offset + lax.broadcasted_iota(jnp.int32, (rows, HEAD_DIM), 0)
        merged = jnp.where(position < first_length, head, tail)
        sorted_all[target, quarter] = merged.astype(sorted_all.dtype)

        @pl.when(shift != 0)
        def _():
            z_copy(target, quarter).start()

        @pl.when(shift == 0)
        def _():
            deliver(sorted_all.at[target, quarter], group, quarter)

    @pl.loop(0, groups * quarters)
    def _(step):
        quarter, shift = step_of(step)
        origin = lax.rem(group + groups - shift, groups)

        @pl.when(shift != 0)
        def _():
            view = placed_all.at[origin, quarter]
            pltpu.make_async_copy(view, view, z_recv.at[origin, quarter]).wait()
            deliver(view, origin, quarter)

    own = head_columns(out_hbm, me)
    pltpu.make_async_copy(sorted_all.at[0, 0], own, own_sem).wait()
    most = out_hbm.at[:, pl.ds(0, (sp_size - 1) * HEAD_DIM)]
    pltpu.make_async_copy(most, most, out_recv).wait()
    others = q_all.at[pl.ds(0, sp_size - 1)]
    for index in range(3):
        pltpu.make_async_copy(others, others, in_send.at[index]).wait()
    pltpu.make_async_copy(others, others, out_send).wait()
    moved = placed_all.at[pl.ds(0, groups - 1)]
    pltpu.make_async_copy(moved, moved, z_send).wait()


def per_device(groups, sp_size, queries, keys, values, clip_lengths, clip_plan):
    rows, width = queries.shape
    quarters = sp_size // groups
    share = rows * quarters
    frames = rows * sp_size
    window = share + rows
    kind = queries.dtype
    hbm = pl.BlockSpec(memory_space=pltpu.HBM)
    smem = pl.BlockSpec(memory_space=pltpu.SMEM)
    return pl.pallas_call(
        functools.partial(fused_kernel, groups, sp_size),
        out_shape=jax.ShapeDtypeStruct((rows, width), kind),
        in_specs=[smem, smem, hbm, hbm, hbm],
        out_specs=hbm,
        scratch_shapes=[
            pltpu.VMEM((sp_size, rows, HEAD_DIM), kind),
            pltpu.VMEM((sp_size + quarters, rows, HEAD_DIM), kind),
            pltpu.VMEM((sp_size + quarters, rows, HEAD_DIM), kind),
            pltpu.VMEM((sp_size, rows, HEAD_DIM), jnp.int32),
            pltpu.VMEM((sp_size, rows, window), kind),
            pltpu.VMEM((sp_size, rows, HEAD_DIM), jnp.float32),
            pltpu.VMEM((share + frames + share, HEAD_DIM), jnp.float32),
            pltpu.VMEM((groups, quarters, rows, HEAD_DIM), kind),
            pltpu.VMEM((groups, quarters, rows, HEAD_DIM), kind),
            pltpu.SemaphoreType.DMA((3,)),
            pltpu.SemaphoreType.DMA((3, sp_size)),
            pltpu.SemaphoreType.DMA,
            pltpu.SemaphoreType.DMA((groups, quarters)),
            pltpu.SemaphoreType.DMA,
            pltpu.SemaphoreType.DMA,
            pltpu.SemaphoreType.DMA,
        ],
        compiler_params=pltpu.CompilerParams(
            collective_id=0, has_side_effects=True, vmem_limit_bytes=56 << 20
        ),
    )(clip_lengths, clip_plan, queries, keys, values)


def solution(mesh):
    rows = P(("grp", "sp"), None)
    return jax.shard_map(
        functools.partial(per_device, mesh.shape["grp"], mesh.shape["sp"]),
        mesh=mesh,
        in_specs=(rows, rows, rows, P("grp", None), P("grp", None)),
        out_specs=rows,
        check_vma=False,
    )
```

```python
import functools
import math

import jax
import jax.numpy as jnp
from jax import lax
from jax.experimental import pallas as pl
from jax.experimental.pallas import tpu as pltpu
from jax.sharding import PartitionSpec as P

HEAD_DIM = 128
MESH = pl.DeviceIdType.MESH
PHASES = 2
CORES = 2
STRIDE = 5
MASKED = -1.0e30


def fused_kernel(
    groups,
    sp_size,
    lens_ref,
    plan_ref,
    q_hbm,
    k_hbm,
    v_hbm,
    out_hbm,
    q_all,
    k_all,
    v_all,
    begin_all,
    prob_all,
    inverse_all,
    mixed_first,
    mixed_second,
    sorted_all,
    placed_all,
    in_send,
    near_send,
    in_recv,
    halo_send,
    halo_recv,
    swap_send,
    swap_recv,
    z_send,
    z_recv,
    out_send,
    own_send,
    out_recv,
):
    rows = q_hbm.shape[0]
    clips = lens_ref.shape[1]
    quarters = sp_size // groups
    chips = sp_size // CORES
    blocks = sp_size // CORES
    held = groups // CORES
    share = rows * quarters
    frames = rows * sp_size
    half = rows * blocks
    window = share + rows
    group = lax.axis_index("grp")
    me = lax.axis_index("sp")
    chip = me // CORES
    core = lax.rem(me, CORES)
    sibling = chip * CORES + 1 - core

    barrier = pltpu.get_barrier_semaphore()

    @pl.loop(1, sp_size)
    def _(t):
        peer = lax.rem(me + t, sp_size)
        pl.semaphore_signal(barrier, inc=1, device_id=(group, peer), device_id_type=MESH)

    @pl.loop(1, groups)
    def _(t):
        peer = lax.rem(group + t, groups)
        pl.semaphore_signal(barrier, inc=1, device_id=(peer, me), device_id_type=MESH)
        pl.semaphore_signal(barrier, inc=1, device_id=(peer, sibling), device_id_type=MESH)

    pl.semaphore_wait(barrier, sp_size - 1 + 2 * (groups - 1))

    def head_columns(array, phase, holder):
        head = phase * chips + holder
        return array.at[:, pl.ds(pl.multiple_of(head * HEAD_DIM, HEAD_DIM), HEAD_DIM)]

    stacks = ((k_hbm, k_all, quarters), (q_hbm, q_all, 0), (v_hbm, v_all, quarters))
    taker = me // blocks
    place = lax.rem(me, blocks)

    def send_heads(phase, index):
        source, stack, pad = stacks[index]
        target = stack.at[phase, pad + place]
        arrived = in_recv.at[phase, index, place]

        @pl.loop(1, chips)
        def _(t):
            holder = lax.rem(chip + t * STRIDE, chips)
            pltpu.make_async_remote_copy(
                src_ref=head_columns(source, phase, holder),
                dst_ref=target,
                send_sem=in_send.at[phase, index],
                recv_sem=arrived,
                device_id=(group, holder * CORES + taker),
                device_id_type=MESH,
            ).start()

        own = head_columns(source, phase, chip)

        @pl.when(taker == core)
        def _():
            pltpu.make_async_copy(own, target, arrived).start()

        @pl.when(taker != core)
        def _():
            pltpu.make_async_remote_copy(
                src_ref=own,
                dst_ref=target,
                send_sem=near_send.at[phase, index],
                recv_sem=arrived,
                device_id=(group, sibling),
                device_id_type=MESH,
            ).start()

    def wait_block(phase, index, block):
        _, stack, pad = stacks[index]
        view = stack.at[phase, pad + block]
        pltpu.make_async_copy(view, view, in_recv.at[phase, index, block]).wait()

    def halo_copy(phase, which, stack):
        return pltpu.make_async_remote_copy(
            src_ref=stack.at[phase, pl.ds(blocks, quarters)],
            dst_ref=stack.at[phase, pl.ds(0, quarters)],
            send_sem=halo_send.at[phase, which],
            recv_sem=halo_recv.at[phase, which],
            device_id=(group, sibling),
            device_id_type=MESH,
        )

    def wait_stack(phase, index, which):
        stack = stacks[index][1]

        @pl.loop(blocks - quarters, blocks)
        def _(block):
            wait_block(phase, index, block)

        @pl.when(core == 0)
        def _():
            halo_copy(phase, which, stack).start()

        @pl.loop(0, blocks - quarters)
        def _(block):
            wait_block(phase, index, block)

    def wait_halo(phase, which, stack):
        @pl.when(core == 1)
        def _():
            halo_copy(phase, which, stack).wait_recv()

    lengths = [lens_ref[0, c] for c in range(clips)]
    plans = [plan_ref[0, c] for c in range(clips)]
    starts = []
    total = jnp.int32(0)
    for c in range(clips):
        starts.append(total)
        total = total + lengths[c]

    for index in range(3):
        send_heads(0, index)

    @pl.when(core == 0)
    def _():
        for phase in range(PHASES):
            for stack in (k_all, v_all):
                stack[phase, 0:quarters] = jnp.zeros((quarters, rows, HEAD_DIM), stack.dtype)

    mixed_all = (mixed_first, mixed_second)
    for mixed in mixed_all:
        mixed[0:share, :] = jnp.zeros((share, HEAD_DIM), jnp.float32)
        mixed[share + frames :, :] = jnp.zeros((share, HEAD_DIM), jnp.float32)

    @pl.loop(0, blocks)
    def _(block):
        first = core * half + block * rows
        position = first + lax.broadcasted_iota(jnp.int32, (rows, HEAD_DIM), 0)
        begin = jnp.zeros((rows, HEAD_DIM), jnp.int32)
        for c in range(1, clips):
            begin = jnp.where(position >= starts[c], starts[c], begin)
        begin_all[block] = begin - (first - share)

    scale = math.log2(math.e) / math.sqrt(HEAD_DIM)
    column = lax.broadcasted_iota(jnp.int32, (rows, window), 1)
    last_key = share + lax.broadcasted_iota(jnp.int32, (rows, window), 0)

    def weigh(phase):
        @pl.loop(0, blocks)
        def _(step):
            block = lax.rem(step + quarters, blocks)

            @pl.when(block == 0)
            def _():
                wait_halo(phase, 0, k_all)

            wait_block(phase, 1, block)
            window_keys = k_all[phase, pl.ds(block, quarters + 1)].reshape(window, HEAD_DIM)
            scores = lax.dot_general(
                q_all[phase, block],
                window_keys,
                (((1,), (1,)), ((), ())),
                preferred_element_type=jnp.float32,
            )
            begin = jnp.broadcast_to(begin_all[block][:, :1], (rows, window))
            allowed = (column >= begin) & (column <= last_key)
            scores = jnp.where(allowed, scores * scale, MASKED)
            highest = jnp.max(scores, axis=1, keepdims=True)
            weights = jnp.exp2(scores - highest)
            totals = jnp.sum(weights, axis=1, keepdims=True)
            inverse_all[block] = jnp.broadcast_to(1.0 / totals, (rows, HEAD_DIM))
            prob_all[block] = weights.astype(prob_all.dtype)

    def swap_copy(phase, first, count):
        view = mixed_all[phase].at[pl.ds(pl.multiple_of(share + first, rows), count), :]
        return pltpu.make_async_remote_copy(
            src_ref=view,
            dst_ref=view,
            send_sem=swap_send.at[phase],
            recv_sem=swap_recv.at[phase],
            device_id=(group, sibling),
            device_id_type=MESH,
        )

    def mix(phase):
        @pl.loop(0, blocks)
        def _(step):
            block = lax.rem(step + quarters, blocks)

            @pl.when(block == 0)
            def _():
                wait_halo(phase, 1, v_all)

            window_values = v_all[phase, pl.ds(block, quarters + 1)].reshape(window, HEAD_DIM)
            mixture = jnp.dot(prob_all[block], window_values, preferred_element_type=jnp.float32)
            first = core * half + block * rows
            mixed_all[phase][pl.ds(pl.multiple_of(share + first, rows), rows), :] = (
                mixture * inverse_all[block]
            )
            swap_copy(phase, first, rows).start()

    def pair_of(target):
        first_start = jnp.int32(0)
        first_length = jnp.int32(0)
        second_start = jnp.int32(0)
        for c in reversed(range(clips)):
            hit = plans[c] == target
            first_start = jnp.where(hit, starts[c], first_start)
            first_length = jnp.where(hit, lengths[c], first_length)
        for c in range(clips):
            second_start = jnp.where(plans[c] == target, starts[c], second_start)
        return first_start, first_length, second_start

    def deliver(phase, block_ref, holder, send_sem, begin):
        target = head_columns(out_hbm, phase, chip)
        remote = pltpu.make_async_remote_copy(
            src_ref=block_ref,
            dst_ref=target,
            send_sem=send_sem,
            recv_sem=out_recv,
            device_id=(group, holder),
            device_id_type=MESH,
        )

        @pl.when(holder != me)
        def _():
            if begin:
                remote.start()
            else:
                remote.wait_send()

        if begin:

            @pl.when(holder == me)
            def _():
                pltpu.make_async_copy(block_ref, target, out_recv).start()

    def regroup_step(step):
        quarter = lax.rem(step // held + chip, quarters)
        slot = lax.rem(step + group, held)
        return quarter, slot, core * held + slot

    def z_copy(phase, slot, target, quarter):
        return pltpu.make_async_remote_copy(
            src_ref=sorted_all.at[phase, slot, quarter],
            dst_ref=placed_all.at[phase, group, quarter // CORES],
            send_sem=z_send.at[phase, slot, quarter],
            recv_sem=z_recv.at[phase, group, quarter // CORES],
            device_id=(target, chip * CORES + lax.rem(quarter, CORES)),
            device_id_type=MESH,
        )

    def send_sorted(phase, begin):
        @pl.loop(0, held * quarters)
        def _(step):
            quarter, slot, target = regroup_step(step)
            if begin:
                first_start, first_length, second_start = pair_of(target)
                offset = quarter * rows
                head = mixed_all[phase][pl.ds(share + first_start + offset, rows), :]
                tail = mixed_all[phase][
                    pl.ds(share + second_start - first_length + offset, rows), :
                ]
                position = offset + lax.broadcasted_iota(jnp.int32, (rows, HEAD_DIM), 0)
                merged = jnp.where(position < first_length, head, tail)
                sorted_all[phase, slot, quarter] = merged.astype(sorted_all.dtype)

            @pl.when(target != group)
            def _():
                if begin:
                    z_copy(phase, slot, target, quarter).start()
                else:
                    z_copy(phase, slot, target, quarter).wait_send()

            @pl.when(target == group)
            def _():
                deliver(
                    phase,
                    sorted_all.at[phase, slot, quarter],
                    group * quarters + quarter,
                    own_send.at[phase, quarter],
                    begin,
                )

    def forward(phase, begin):
        rounds = quarters // CORES
        parity = lax.rem(core + chip, CORES)

        @pl.loop(0, rounds * (groups - 1))
        def _(step):
            turn = step // (groups - 1)
            near = lax.rem(step, groups - 1) + 1
            odd = lax.rem(near, 2)
            hops = (near + 1) // 2
            shift = odd * hops + (1 - odd) * (groups - hops)
            origin = lax.rem(group + shift, groups)
            quarter = lax.rem(parity + CORES * turn + chip, quarters)
            kept = quarter // CORES
            view = placed_all.at[phase, origin, kept]
            if begin:
                pltpu.make_async_copy(view, view, z_recv.at[phase, origin, kept]).wait()
            deliver(
                phase, view, origin * quarters + quarter, out_send.at[phase, origin, kept], begin
            )

    for phase in range(PHASES):
        wait_stack(phase, 0, 0)
        if phase + 1 < PHASES:
            for index in range(3):
                send_heads(phase + 1, index)
        weigh(phase)
        wait_stack(phase, 2, 1)
        mix(phase)
        swap_copy(phase, (1 - core) * half, half).wait_recv()
        send_sorted(phase, True)
    for phase in range(PHASES):
        forward(phase, True)

    for phase in range(PHASES):
        for index in range(3):
            others = q_all.at[phase, pl.ds(0, chips - 1)]
            pltpu.make_async_copy(others, others, in_send.at[phase, index]).wait()

            @pl.when(taker != core)
            def _():
                one = q_all.at[phase, 0]
                pltpu.make_async_copy(one, one, near_send.at[phase, index]).wait()

        @pl.when(core == 0)
        def _():
            halo_copy(phase, 0, k_all).wait_send()
            halo_copy(phase, 1, v_all).wait_send()

        swap_copy(phase, core * half, half).wait_send()
        send_sorted(phase, False)
        forward(phase, False)
    pltpu.make_async_copy(out_hbm, out_hbm, out_recv).wait()


def per_device(groups, sp_size, queries, keys, values, clip_lengths, clip_plan):
    rows, width = queries.shape
    quarters = sp_size // groups
    blocks = sp_size // CORES
    held = groups // CORES
    kept = quarters // CORES
    share = rows * quarters
    frames = rows * sp_size
    window = share + rows
    kind = queries.dtype
    hbm = pl.BlockSpec(memory_space=pltpu.HBM)
    smem = pl.BlockSpec(memory_space=pltpu.SMEM)
    dma = pltpu.SemaphoreType.DMA
    return pl.pallas_call(
        functools.partial(fused_kernel, groups, sp_size),
        out_shape=jax.ShapeDtypeStruct((rows, width), kind),
        in_specs=[smem, smem, hbm, hbm, hbm],
        out_specs=hbm,
        scratch_shapes=[
            pltpu.VMEM((PHASES, blocks, rows, HEAD_DIM), kind),
            pltpu.VMEM((PHASES, blocks + quarters, rows, HEAD_DIM), kind),
            pltpu.VMEM((PHASES, blocks + quarters, rows, HEAD_DIM), kind),
            pltpu.VMEM((blocks, rows, HEAD_DIM), jnp.int32),
            pltpu.VMEM((blocks, rows, window), kind),
            pltpu.VMEM((blocks, rows, HEAD_DIM), jnp.float32),
            pltpu.VMEM((share + frames + share, HEAD_DIM), jnp.float32),
            pltpu.VMEM((share + frames + share, HEAD_DIM), jnp.float32),
            pltpu.VMEM((PHASES, held, quarters, rows, HEAD_DIM), kind),
            pltpu.VMEM((PHASES, groups, kept, rows, HEAD_DIM), kind),
            dma((PHASES, 3)),
            dma((PHASES, 3)),
            dma((PHASES, 3, blocks)),
            dma((PHASES, 2)),
            dma((PHASES, 2)),
            dma((PHASES,)),
            dma((PHASES,)),
            dma((PHASES, held, quarters)),
            dma((PHASES, groups, kept)),
            dma((PHASES, groups, kept)),
            dma((PHASES, quarters)),
            dma,
        ],
        compiler_params=pltpu.CompilerParams(
            collective_id=0, has_side_effects=True, vmem_limit_bytes=56 << 20
        ),
    )(clip_lengths, clip_plan, queries, keys, values)


def solution(mesh):
    rows = P(("grp", "sp"), None)
    return jax.shard_map(
        functools.partial(per_device, mesh.shape["grp"], mesh.shape["sp"]),
        mesh=mesh,
        in_specs=(rows, rows, rows, P("grp", None), P("grp", None)),
        out_specs=rows,
        check_vma=False,
    )
```

```python
import functools
import math

import jax
import jax.numpy as jnp
from jax import lax
from jax.experimental import pallas as pl
from jax.experimental.pallas import tpu as pltpu
from jax.sharding import PartitionSpec as P

HEAD_DIM = 128
MESH = pl.DeviceIdType.MESH
PHASES = 2
CORES = 2
STRIDE = 5
MASKED = -1.0e30


def fused_kernel(
    groups,
    sp_size,
    lens_ref,
    plan_ref,
    q_hbm,
    k_hbm,
    v_hbm,
    out_hbm,
    q_all,
    k_all,
    v_all,
    begin_all,
    prob_all,
    inverse_all,
    mixed_first,
    mixed_second,
    sorted_all,
    placed_all,
    in_send,
    near_send,
    in_recv,
    halo_send,
    halo_recv,
    swap_send,
    swap_recv,
    z_send,
    z_recv,
    out_send,
    own_send,
    out_recv,
):
    rows = q_hbm.shape[0]
    clips = lens_ref.shape[1]
    quarters = sp_size // groups
    chips = sp_size // CORES
    blocks = sp_size // CORES
    held = groups // CORES
    share = rows * quarters
    frames = rows * sp_size
    half = rows * blocks
    window = share + rows
    group = lax.axis_index("grp")
    me = lax.axis_index("sp")
    chip = me // CORES
    core = lax.rem(me, CORES)
    sibling = chip * CORES + 1 - core

    barrier = pltpu.get_barrier_semaphore()

    @pl.loop(1, sp_size)
    def _(t):
        peer = lax.rem(me + t, sp_size)
        pl.semaphore_signal(barrier, inc=1, device_id=(group, peer), device_id_type=MESH)

    @pl.loop(1, groups)
    def _(t):
        peer = lax.rem(group + t, groups)
        pl.semaphore_signal(barrier, inc=1, device_id=(peer, me), device_id_type=MESH)
        pl.semaphore_signal(barrier, inc=1, device_id=(peer, sibling), device_id_type=MESH)

    pl.semaphore_wait(barrier, sp_size - 1 + 2 * (groups - 1))

    def head_columns(array, phase, holder):
        head = phase * chips + holder
        return array.at[:, pl.ds(pl.multiple_of(head * HEAD_DIM, HEAD_DIM), HEAD_DIM)]

    stacks = ((k_hbm, k_all, quarters), (q_hbm, q_all, 0), (v_hbm, v_all, quarters))
    taker = me // blocks
    place = lax.rem(me, blocks)

    def send_heads(phase, index):
        source, stack, pad = stacks[index]
        target = stack.at[phase, pad + place]
        arrived = in_recv.at[phase, index, place]

        @pl.loop(1, chips)
        def _(t):
            holder = lax.rem(chip + t * STRIDE, chips)
            pltpu.make_async_remote_copy(
                src_ref=head_columns(source, phase, holder),
                dst_ref=target,
                send_sem=in_send.at[phase, index],
                recv_sem=arrived,
                device_id=(group, holder * CORES + taker),
                device_id_type=MESH,
            ).start()

        own = head_columns(source, phase, chip)

        @pl.when(taker == core)
        def _():
            pltpu.make_async_copy(own, target, arrived).start()

        @pl.when(taker != core)
        def _():
            pltpu.make_async_remote_copy(
                src_ref=own,
                dst_ref=target,
                send_sem=near_send.at[phase, index],
                recv_sem=arrived,
                device_id=(group, sibling),
                device_id_type=MESH,
            ).start()

    def wait_block(phase, index, block):
        _, stack, pad = stacks[index]
        view = stack.at[phase, pad + block]
        pltpu.make_async_copy(view, view, in_recv.at[phase, index, block]).wait()

    def halo_copy(phase, which, stack):
        return pltpu.make_async_remote_copy(
            src_ref=stack.at[phase, pl.ds(blocks, quarters)],
            dst_ref=stack.at[phase, pl.ds(0, quarters)],
            send_sem=halo_send.at[phase, which],
            recv_sem=halo_recv.at[phase, which],
            device_id=(group, sibling),
            device_id_type=MESH,
        )

    def wait_stack(phase, index, which):
        stack = stacks[index][1]

        @pl.loop(blocks - quarters, blocks)
        def _(block):
            wait_block(phase, index, block)

        @pl.when(core == 0)
        def _():
            halo_copy(phase, which, stack).start()

        @pl.loop(0, blocks - quarters)
        def _(block):
            wait_block(phase, index, block)

    def wait_halo(phase, which, stack):
        @pl.when(core == 1)
        def _():
            halo_copy(phase, which, stack).wait_recv()

    lengths = [lens_ref[0, c] for c in range(clips)]
    plans = [plan_ref[0, c] for c in range(clips)]
    starts = []
    total = jnp.int32(0)
    for c in range(clips):
        starts.append(total)
        total = total + lengths[c]

    for index in range(3):
        send_heads(0, index)

    @pl.when(core == 0)
    def _():
        for phase in range(PHASES):
            for stack in (k_all, v_all):
                stack[phase, 0:quarters] = jnp.zeros((quarters, rows, HEAD_DIM), stack.dtype)

    mixed_all = (mixed_first, mixed_second)
    for mixed in mixed_all:
        mixed[0:share, :] = jnp.zeros((share, HEAD_DIM), jnp.float32)
        mixed[share + frames :, :] = jnp.zeros((share, HEAD_DIM), jnp.float32)

    @pl.loop(0, blocks)
    def _(block):
        first = core * half + block * rows
        position = first + lax.broadcasted_iota(jnp.int32, (rows, HEAD_DIM), 0)
        begin = jnp.zeros((rows, HEAD_DIM), jnp.int32)
        for c in range(1, clips):
            begin = jnp.where(position >= starts[c], starts[c], begin)
        begin_all[block] = begin - (first - share)

    scale = math.log2(math.e) / math.sqrt(HEAD_DIM)
    column = lax.broadcasted_iota(jnp.int32, (rows, window), 1)
    last_key = share + lax.broadcasted_iota(jnp.int32, (rows, window), 0)

    def weigh(phase):
        @pl.loop(0, blocks)
        def _(step):
            block = lax.rem(step + quarters, blocks)

            @pl.when(block == 0)
            def _():
                wait_halo(phase, 0, k_all)

            wait_block(phase, 1, block)
            window_keys = k_all[phase, pl.ds(block, quarters + 1)].reshape(window, HEAD_DIM)
            scores = lax.dot_general(
                q_all[phase, block],
                window_keys,
                (((1,), (1,)), ((), ())),
                preferred_element_type=jnp.float32,
            )
            begin = jnp.broadcast_to(begin_all[block][:, :1], (rows, window))
            allowed = (column >= begin) & (column <= last_key)
            scores = jnp.where(allowed, scores * scale, MASKED)
            highest = jnp.max(scores, axis=1, keepdims=True)
            weights = jnp.exp2(scores - highest)
            totals = jnp.sum(weights, axis=1, keepdims=True)
            inverse_all[block] = jnp.broadcast_to(1.0 / totals, (rows, HEAD_DIM))
            prob_all[block] = weights.astype(prob_all.dtype)

    def swap_copy(phase, first, count):
        view = mixed_all[phase].at[pl.ds(pl.multiple_of(share + first, rows), count), :]
        return pltpu.make_async_remote_copy(
            src_ref=view,
            dst_ref=view,
            send_sem=swap_send.at[phase],
            recv_sem=swap_recv.at[phase],
            device_id=(group, sibling),
            device_id_type=MESH,
        )

    def mix(phase):
        @pl.loop(0, blocks)
        def _(step):
            block = lax.rem(step + quarters, blocks)

            @pl.when(block == 0)
            def _():
                wait_halo(phase, 1, v_all)

            window_values = v_all[phase, pl.ds(block, quarters + 1)].reshape(window, HEAD_DIM)
            mixture = jnp.dot(prob_all[block], window_values, preferred_element_type=jnp.float32)
            first = core * half + block * rows
            mixed_all[phase][pl.ds(pl.multiple_of(share + first, rows), rows), :] = (
                mixture * inverse_all[block]
            )
            swap_copy(phase, first, rows).start()

    def pair_of(target):
        first_start = jnp.int32(0)
        first_length = jnp.int32(0)
        second_start = jnp.int32(0)
        for c in reversed(range(clips)):
            hit = plans[c] == target
            first_start = jnp.where(hit, starts[c], first_start)
            first_length = jnp.where(hit, lengths[c], first_length)
        for c in range(clips):
            second_start = jnp.where(plans[c] == target, starts[c], second_start)
        return first_start, first_length, second_start

    def deliver(phase, block_ref, holder, send_sem, begin):
        target = head_columns(out_hbm, phase, chip)
        remote = pltpu.make_async_remote_copy(
            src_ref=block_ref,
            dst_ref=target,
            send_sem=send_sem,
            recv_sem=out_recv,
            device_id=(group, holder),
            device_id_type=MESH,
        )

        @pl.when(holder != me)
        def _():
            if begin:
                remote.start()
            else:
                remote.wait_send()

        if begin:

            @pl.when(holder == me)
            def _():
                pltpu.make_async_copy(block_ref, target, out_recv).start()

    def regroup_step(step):
        quarter = lax.rem(step // held + chip, quarters)
        slot = lax.rem(step + group, held)
        return quarter, slot, core * held + slot

    def z_copy(phase, slot, target, quarter):
        return pltpu.make_async_remote_copy(
            src_ref=sorted_all.at[phase, slot, quarter],
            dst_ref=placed_all.at[phase, group, quarter // CORES],
            send_sem=z_send.at[phase, slot, quarter],
            recv_sem=z_recv.at[phase, group, quarter // CORES],
            device_id=(target, chip * CORES + lax.rem(quarter, CORES)),
            device_id_type=MESH,
        )

    def send_sorted(phase, begin):
        @pl.loop(0, held * quarters)
        def _(step):
            quarter, slot, target = regroup_step(step)
            if begin:
                first_start, first_length, second_start = pair_of(target)
                offset = quarter * rows
                head = mixed_all[phase][pl.ds(share + first_start + offset, rows), :]
                tail = mixed_all[phase][
                    pl.ds(share + second_start - first_length + offset, rows), :
                ]
                position = offset + lax.broadcasted_iota(jnp.int32, (rows, HEAD_DIM), 0)
                merged = jnp.where(position < first_length, head, tail)
                sorted_all[phase, slot, quarter] = merged.astype(sorted_all.dtype)

            @pl.when(target != group)
            def _():
                if begin:
                    z_copy(phase, slot, target, quarter).start()
                else:
                    z_copy(phase, slot, target, quarter).wait_send()

            @pl.when(target == group)
            def _():
                deliver(
                    phase,
                    sorted_all.at[phase, slot, quarter],
                    group * quarters + quarter,
                    own_send.at[phase, quarter],
                    begin,
                )

    def forward(phase, begin):
        rounds = quarters // CORES
        parity = lax.rem(core + chip, CORES)

        @pl.loop(0, rounds * (groups - 1))
        def _(step):
            turn = step // (groups - 1)
            near = lax.rem(step, groups - 1) + 1
            odd = lax.rem(near, 2)
            hops = (near + 1) // 2
            shift = odd * hops + (1 - odd) * (groups - hops)
            origin = lax.rem(group + shift, groups)
            quarter = lax.rem(parity + CORES * turn + chip, quarters)
            kept = quarter // CORES
            view = placed_all.at[phase, origin, kept]
            if begin:
                pltpu.make_async_copy(view, view, z_recv.at[phase, origin, kept]).wait()
            deliver(
                phase, view, origin * quarters + quarter, out_send.at[phase, origin, kept], begin
            )

    for phase in range(PHASES):
        wait_stack(phase, 0, 0)
        if phase + 1 < PHASES:
            for index in range(3):
                send_heads(phase + 1, index)
        weigh(phase)
        if phase == 1:
            forward(0, True)
        wait_stack(phase, 2, 1)
        mix(phase)
        swap_copy(phase, (1 - core) * half, half).wait_recv()
        send_sorted(phase, True)
    forward(1, True)

    for phase in range(PHASES):
        for index in range(3):
            others = q_all.at[phase, pl.ds(0, chips - 1)]
            pltpu.make_async_copy(others, others, in_send.at[phase, index]).wait()

            @pl.when(taker != core)
            def _():
                one = q_all.at[phase, 0]
                pltpu.make_async_copy(one, one, near_send.at[phase, index]).wait()

        @pl.when(core == 0)
        def _():
            halo_copy(phase, 0, k_all).wait_send()
            halo_copy(phase, 1, v_all).wait_send()

        swap_copy(phase, core * half, half).wait_send()
        send_sorted(phase, False)
        forward(phase, False)
    pltpu.make_async_copy(out_hbm, out_hbm, out_recv).wait()


def per_device(groups, sp_size, queries, keys, values, clip_lengths, clip_plan):
    rows, width = queries.shape
    quarters = sp_size // groups
    blocks = sp_size // CORES
    held = groups // CORES
    kept = quarters // CORES
    share = rows * quarters
    frames = rows * sp_size
    window = share + rows
    kind = queries.dtype
    hbm = pl.BlockSpec(memory_space=pltpu.HBM)
    smem = pl.BlockSpec(memory_space=pltpu.SMEM)
    dma = pltpu.SemaphoreType.DMA
    return pl.pallas_call(
        functools.partial(fused_kernel, groups, sp_size),
        out_shape=jax.ShapeDtypeStruct((rows, width), kind),
        in_specs=[smem, smem, hbm, hbm, hbm],
        out_specs=hbm,
        scratch_shapes=[
            pltpu.VMEM((PHASES, blocks, rows, HEAD_DIM), kind),
            pltpu.VMEM((PHASES, blocks + quarters, rows, HEAD_DIM), kind),
            pltpu.VMEM((PHASES, blocks + quarters, rows, HEAD_DIM), kind),
            pltpu.VMEM((blocks, rows, HEAD_DIM), jnp.int32),
            pltpu.VMEM((blocks, rows, window), kind),
            pltpu.VMEM((blocks, rows, HEAD_DIM), jnp.float32),
            pltpu.VMEM((share + frames + share, HEAD_DIM), jnp.float32),
            pltpu.VMEM((share + frames + share, HEAD_DIM), jnp.float32),
            pltpu.VMEM((PHASES, held, quarters, rows, HEAD_DIM), kind),
            pltpu.VMEM((PHASES, groups, kept, rows, HEAD_DIM), kind),
            dma((PHASES, 3)),
            dma((PHASES, 3)),
            dma((PHASES, 3, blocks)),
            dma((PHASES, 2)),
            dma((PHASES, 2)),
            dma((PHASES,)),
            dma((PHASES,)),
            dma((PHASES, held, quarters)),
            dma((PHASES, groups, kept)),
            dma((PHASES, groups, kept)),
            dma((PHASES, quarters)),
            dma,
        ],
        compiler_params=pltpu.CompilerParams(
            collective_id=0, has_side_effects=True, vmem_limit_bytes=56 << 20
        ),
    )(clip_lengths, clip_plan, queries, keys, values)


def solution(mesh):
    rows = P(("grp", "sp"), None)
    return jax.shard_map(
        functools.partial(per_device, mesh.shape["grp"], mesh.shape["sp"]),
        mesh=mesh,
        in_specs=(rows, rows, rows, P("grp", None), P("grp", None)),
        out_specs=rows,
        check_vma=False,
    )
```

```python
import functools
import math

import jax
import jax.numpy as jnp
from jax import lax
from jax.experimental import pallas as pl
from jax.experimental.pallas import tpu as pltpu
from jax.sharding import PartitionSpec as P

HEAD_DIM = 128
MESH = pl.DeviceIdType.MESH
PHASES = 2
CORES = 2
STRIDE = 5
MASKED = -1.0e30


def fused_kernel(
    groups,
    sp_size,
    lens_ref,
    plan_ref,
    q_hbm,
    k_hbm,
    v_hbm,
    out_hbm,
    q_all,
    k_all,
    v_all,
    begin_all,
    prob_all,
    inverse_all,
    mixed_first,
    mixed_second,
    sorted_all,
    placed_all,
    in_send,
    near_send,
    in_recv,
    halo_send,
    halo_recv,
    swap_send,
    swap_recv,
    z_send,
    z_recv,
    out_send,
    own_send,
    out_recv,
):
    rows = q_hbm.shape[0]
    clips = lens_ref.shape[1]
    quarters = sp_size // groups
    chips = sp_size // CORES
    blocks = sp_size // CORES
    held = groups // CORES
    share = rows * quarters
    frames = rows * sp_size
    half = rows * blocks
    window = share + rows
    group = lax.axis_index("grp")
    me = lax.axis_index("sp")
    chip = me // CORES
    core = lax.rem(me, CORES)
    sibling = chip * CORES + 1 - core

    barrier = pltpu.get_barrier_semaphore()

    @pl.loop(1, sp_size)
    def _(t):
        peer = lax.rem(me + t, sp_size)
        pl.semaphore_signal(barrier, inc=1, device_id=(group, peer), device_id_type=MESH)

    @pl.loop(1, groups)
    def _(t):
        peer = lax.rem(group + t, groups)
        pl.semaphore_signal(barrier, inc=1, device_id=(peer, me), device_id_type=MESH)
        pl.semaphore_signal(barrier, inc=1, device_id=(peer, sibling), device_id_type=MESH)

    pl.semaphore_wait(barrier, sp_size - 1 + 2 * (groups - 1))

    def head_columns(array, phase, holder):
        head = phase * chips + holder
        return array.at[:, pl.ds(pl.multiple_of(head * HEAD_DIM, HEAD_DIM), HEAD_DIM)]

    stacks = ((k_hbm, k_all, quarters), (q_hbm, q_all, 0), (v_hbm, v_all, quarters))
    taker = me // blocks
    place = lax.rem(me, blocks)

    def send_heads(phase, index):
        source, stack, pad = stacks[index]
        target = stack.at[phase, pad + place]
        arrived = in_recv.at[phase, index, place]

        for dx, dy in [(2, 2), (2, 1), (1, 2), (2, -1), (-1, 2), (1, 1), (-1, -1), (1, -1), (-1, 1), (2, 0), (0, 2), (1, 0), (0, 1), (-1, 0), (0, -1)]:
            sign = 1 - 2 * core if True else 1
            holder = lax.rem(chip // 4 + sign * dy + 8, 4) * 4 + lax.rem(lax.rem(chip, 4) + sign * dx + 8, 4)
            pltpu.make_async_remote_copy(
                src_ref=head_columns(source, phase, holder),
                dst_ref=target,
                send_sem=in_send.at[phase, index],
                recv_sem=arrived,
                device_id=(group, holder * CORES + taker),
                device_id_type=MESH,
            ).start()

        own = head_columns(source, phase, chip)

        @pl.when(taker == core)
        def _():
            pltpu.make_async_copy(own, target, arrived).start()

        @pl.when(taker != core)
        def _():
            pltpu.make_async_remote_copy(
                src_ref=own,
                dst_ref=target,
                send_sem=near_send.at[phase, index],
                recv_sem=arrived,
                device_id=(group, sibling),
                device_id_type=MESH,
            ).start()

    def wait_block(phase, index, block):
        _, stack, pad = stacks[index]
        view = stack.at[phase, pad + block]
        pltpu.make_async_copy(view, view, in_recv.at[phase, index, block]).wait()

    def halo_copy(phase, which, stack):
        return pltpu.make_async_remote_copy(
            src_ref=stack.at[phase, pl.ds(blocks, quarters)],
            dst_ref=stack.at[phase, pl.ds(0, quarters)],
            send_sem=halo_send.at[phase, which],
            recv_sem=halo_recv.at[phase, which],
            device_id=(group, sibling),
            device_id_type=MESH,
        )

    def wait_stack(phase, index, which):
        stack = stacks[index][1]

        @pl.loop(blocks - quarters, blocks)
        def _(block):
            wait_block(phase, index, block)

        @pl.when(core == 0)
        def _():
            halo_copy(phase, which, stack).start()

        @pl.loop(0, blocks - quarters)
        def _(block):
            wait_block(phase, index, block)

    def wait_halo(phase, which, stack):
        @pl.when(core == 1)
        def _():
            halo_copy(phase, which, stack).wait_recv()

    lengths = [lens_ref[0, c] for c in range(clips)]
    plans = [plan_ref[0, c] for c in range(clips)]
    starts = []
    total = jnp.int32(0)
    for c in range(clips):
        starts.append(total)
        total = total + lengths[c]

    for index in range(3):
        send_heads(0, index)

    @pl.when(core == 0)
    def _():
        for phase in range(PHASES):
            for stack in (k_all, v_all):
                stack[phase, 0:quarters] = jnp.zeros((quarters, rows, HEAD_DIM), stack.dtype)

    mixed_all = (mixed_first, mixed_second)
    for mixed in mixed_all:
        mixed[0:share, :] = jnp.zeros((share, HEAD_DIM), jnp.float32)
        mixed[share + frames :, :] = jnp.zeros((share, HEAD_DIM), jnp.float32)

    @pl.loop(0, blocks)
    def _(block):
        first = core * half + block * rows
        position = first + lax.broadcasted_iota(jnp.int32, (rows, HEAD_DIM), 0)
        begin = jnp.zeros((rows, HEAD_DIM), jnp.int32)
        for c in range(1, clips):
            begin = jnp.where(position >= starts[c], starts[c], begin)
        begin_all[block] = begin - (first - share)

    def pair_of(target):
        first_start = jnp.int32(0)
        first_length = jnp.int32(0)
        second_start = jnp.int32(0)
        for c in reversed(range(clips)):
            hit = plans[c] == target
            first_start = jnp.where(hit, starts[c], first_start)
            first_length = jnp.where(hit, lengths[c], first_length)
        for c in range(clips):
            second_start = jnp.where(plans[c] == target, starts[c], second_start)
        return first_start, first_length, second_start

    pairs = [pair_of(core * held + slot) for slot in range(held)]

    def pick(slot):
        found = pairs[0]
        for other in range(1, held):
            found = [jnp.where(slot == other, a, b) for a, b in zip(pairs[other], found)]
        return found

    scale = math.log2(math.e) / math.sqrt(HEAD_DIM)
    column = lax.broadcasted_iota(jnp.int32, (rows, window), 1)
    last_key = share + lax.broadcasted_iota(jnp.int32, (rows, window), 0)

    def weigh(phase):
        @pl.loop(0, blocks)
        def _(step):
            block = lax.rem(step + quarters, blocks)

            @pl.when(block == 0)
            def _():
                wait_halo(phase, 0, k_all)

            wait_block(phase, 1, block)
            window_keys = k_all[phase, pl.ds(block, quarters + 1)].reshape(window, HEAD_DIM)
            scores = lax.dot_general(
                q_all[phase, block],
                window_keys,
                (((1,), (1,)), ((), ())),
                preferred_element_type=jnp.float32,
            )
            begin = jnp.broadcast_to(begin_all[block][:, :1], (rows, window))
            allowed = (column >= begin) & (column <= last_key)
            scores = jnp.where(allowed, scores * scale, MASKED)
            highest = jnp.max(scores, axis=1, keepdims=True)
            weights = jnp.exp2(scores - highest)
            totals = jnp.sum(weights, axis=1, keepdims=True)
            inverse_all[block] = jnp.broadcast_to(1.0 / totals, (rows, HEAD_DIM))
            prob_all[block] = weights.astype(prob_all.dtype)

    def swap_copy(phase, first, count):
        view = mixed_all[phase].at[pl.ds(pl.multiple_of(share + first, rows), count), :]
        return pltpu.make_async_remote_copy(
            src_ref=view,
            dst_ref=view,
            send_sem=swap_send.at[phase],
            recv_sem=swap_recv.at[phase],
            device_id=(group, sibling),
            device_id_type=MESH,
        )

    def mix(phase):
        @pl.loop(0, blocks)
        def _(step):
            block = lax.rem(step + quarters, blocks)

            @pl.when(block == 0)
            def _():
                wait_halo(phase, 1, v_all)

            window_values = v_all[phase, pl.ds(block, quarters + 1)].reshape(window, HEAD_DIM)
            mixture = jnp.dot(prob_all[block], window_values, preferred_element_type=jnp.float32)
            first = core * half + block * rows
            mixed_all[phase][pl.ds(pl.multiple_of(share + first, rows), rows), :] = (
                mixture * inverse_all[block]
            )
            swap_copy(phase, first, rows).start()

    def deliver(phase, block_ref, holder, send_sem, begin):
        target = head_columns(out_hbm, phase, chip)
        remote = pltpu.make_async_remote_copy(
            src_ref=block_ref,
            dst_ref=target,
            send_sem=send_sem,
            recv_sem=out_recv,
            device_id=(group, holder),
            device_id_type=MESH,
        )

        @pl.when(holder != me)
        def _():
            if begin:
                remote.start()
            else:
                remote.wait_send()

        if begin:

            @pl.when(holder == me)
            def _():
                pltpu.make_async_copy(block_ref, target, out_recv).start()

    def regroup_step(step):
        quarter = lax.rem(step // held + chip, quarters)
        slot = lax.rem(step + group, held)
        return quarter, slot, core * held + slot

    def z_copy(phase, slot, target, quarter):
        return pltpu.make_async_remote_copy(
            src_ref=sorted_all.at[phase, slot, quarter],
            dst_ref=placed_all.at[phase, group, quarter // CORES],
            send_sem=z_send.at[phase, slot, quarter],
            recv_sem=z_recv.at[phase, group, quarter // CORES],
            device_id=(target, chip * CORES + lax.rem(quarter, CORES)),
            device_id_type=MESH,
        )

    def send_sorted(phase, begin):
        @pl.loop(0, held * quarters)
        def _(step):
            quarter, slot, target = regroup_step(step)
            if begin:
                first_start, first_length, second_start = pick(slot)
                offset = quarter * rows
                head = mixed_all[phase][pl.ds(share + first_start + offset, rows), :]
                tail = mixed_all[phase][
                    pl.ds(share + second_start - first_length + offset, rows), :
                ]
                position = offset + lax.broadcasted_iota(jnp.int32, (rows, HEAD_DIM), 0)
                merged = jnp.where(position < first_length, head, tail)
                sorted_all[phase, slot, quarter] = merged.astype(sorted_all.dtype)

            @pl.when(target != group)
            def _():
                if begin:
                    z_copy(phase, slot, target, quarter).start()
                else:
                    z_copy(phase, slot, target, quarter).wait_send()

            @pl.when(target == group)
            def _():
                deliver(
                    phase,
                    sorted_all.at[phase, slot, quarter],
                    group * quarters + quarter,
                    own_send.at[phase, quarter],
                    begin,
                )

    def forward(phase, begin):
        rounds = quarters // CORES
        parity = lax.rem(core + chip, CORES)

        @pl.loop(0, rounds * (groups - 1))
        def _(step):
            turn = step // (groups - 1)
            near = lax.rem(step, groups - 1) + 1
            odd = lax.rem(near, 2)
            hops = (near + 1) // 2
            shift = odd * hops + (1 - odd) * (groups - hops)
            origin = lax.rem(group + shift, groups)
            quarter = lax.rem(parity + CORES * turn + chip, quarters)
            kept = quarter // CORES
            view = placed_all.at[phase, origin, kept]
            if begin:
                pltpu.make_async_copy(view, view, z_recv.at[phase, origin, kept]).wait()
            deliver(
                phase, view, origin * quarters + quarter, out_send.at[phase, origin, kept], begin
            )

    for phase in range(PHASES):
        wait_stack(phase, 0, 0)
        if phase + 1 < PHASES:
            for index in range(3):
                send_heads(phase + 1, index)
        weigh(phase)
        if phase == 1:
            forward(0, True)
        wait_stack(phase, 2, 1)
        mix(phase)
        swap_copy(phase, (1 - core) * half, half).wait_recv()
        send_sorted(phase, True)
    forward(1, True)

    for phase in range(PHASES):
        for index in range(3):
            others = q_all.at[phase, pl.ds(0, chips - 1)]
            pltpu.make_async_copy(others, others, in_send.at[phase, index]).wait()

            @pl.when(taker != core)
            def _():
                one = q_all.at[phase, 0]
                pltpu.make_async_copy(one, one, near_send.at[phase, index]).wait()

        @pl.when(core == 0)
        def _():
            halo_copy(phase, 0, k_all).wait_send()
            halo_copy(phase, 1, v_all).wait_send()

        swap_copy(phase, core * half, half).wait_send()
        send_sorted(phase, False)
        forward(phase, False)
    pltpu.make_async_copy(out_hbm, out_hbm, out_recv).wait()


def per_device(groups, sp_size, queries, keys, values, clip_lengths, clip_plan):
    rows, width = queries.shape
    quarters = sp_size // groups
    blocks = sp_size // CORES
    held = groups // CORES
    kept = quarters // CORES
    share = rows * quarters
    frames = rows * sp_size
    window = share + rows
    kind = queries.dtype
    hbm = pl.BlockSpec(memory_space=pltpu.HBM)
    smem = pl.BlockSpec(memory_space=pltpu.SMEM)
    dma = pltpu.SemaphoreType.DMA
    return pl.pallas_call(
        functools.partial(fused_kernel, groups, sp_size),
        out_shape=jax.ShapeDtypeStruct((rows, width), kind),
        in_specs=[smem, smem, hbm, hbm, hbm],
        out_specs=hbm,
        scratch_shapes=[
            pltpu.VMEM((PHASES, blocks, rows, HEAD_DIM), kind),
            pltpu.VMEM((PHASES, blocks + quarters, rows, HEAD_DIM), kind),
            pltpu.VMEM((PHASES, blocks + quarters, rows, HEAD_DIM), kind),
            pltpu.VMEM((blocks, rows, HEAD_DIM), jnp.int32),
            pltpu.VMEM((blocks, rows, window), kind),
            pltpu.VMEM((blocks, rows, HEAD_DIM), jnp.float32),
            pltpu.VMEM((share + frames + share, HEAD_DIM), jnp.float32),
            pltpu.VMEM((share + frames + share, HEAD_DIM), jnp.float32),
            pltpu.VMEM((PHASES, held, quarters, rows, HEAD_DIM), kind),
            pltpu.VMEM((PHASES, groups, kept, rows, HEAD_DIM), kind),
            dma((PHASES, 3)),
            dma((PHASES, 3)),
            dma((PHASES, 3, blocks)),
            dma((PHASES, 2)),
            dma((PHASES, 2)),
            dma((PHASES,)),
            dma((PHASES,)),
            dma((PHASES, held, quarters)),
            dma((PHASES, groups, kept)),
            dma((PHASES, groups, kept)),
            dma((PHASES, quarters)),
            dma,
        ],
        compiler_params=pltpu.CompilerParams(
            collective_id=0, has_side_effects=True, vmem_limit_bytes=56 << 20
        ),
    )(clip_lengths, clip_plan, queries, keys, values)


def solution(mesh):
    rows = P(("grp", "sp"), None)
    return jax.shard_map(
        functools.partial(per_device, mesh.shape["grp"], mesh.shape["sp"]),
        mesh=mesh,
        in_specs=(rows, rows, rows, P("grp", None), P("grp", None)),
        out_specs=rows,
        check_vma=False,
    )
```
